512 devices in a mesh: pair: 64 (over z_hi, y, core), fft: 8 (over x, z_lo).
Axes of the slice: x: 4, y: 8, z: 8 (z_hi: 4, z_lo: 2; z = z_hi * 2 + z_lo), core: 2. Of those that a mesh axis runs over, the one named last changes fastest.
Arguments:
- psi_val: bfloat16 [384, 64, 64, 128], P('pair', 'fft'), may hold values from -6 to 6
- psi_cond: bfloat16 [384, 64, 64, 128], P('pair', 'fft'), may hold values from -6 to 6
- pair_bands: int32 [256, 2], P('pair'), may hold values from 0 to 5
- eps_val: float32 [384], P('pair'), may hold values from -4.125 to -0.125
- eps_cond: float32 [384], P('pair'), may hold values from 0.125 to 4.125
- g_map: int32 [10240], P('fft'), may hold values from 0 to 262143, as said below
Outputs:
- chi0: float32 [2, 10240, 10240], P(None, 'pair', 'fft')
The draws below stay inside these ranges and needn't reach their ends.
Inputs may be any that keep to these rules, and one draw needn't show every extreme that they name: `pair_bands`: values name bands of the pair's own group. `g_map`: distinct values; the plane waves of block f (entries f * 1280 to (f + 1) * 1280 - 1) all lie on grid points whose second coordinate y is within f * 8 to (f + 1) * 8 - 1.
All inputs are finite; a program needn't handle non-finite values.
Results may differ from the reference program's by a relative error of at most 0.017.
Values may be sent and summed in bfloat16 or wider, within the bound.
No kernel may reach another device: no remote copies, remote signals or barrier semaphores. Data moves between devices by JAX's collectives and lax.ppermute only.
A program may use at most 64 MiB of HBM per device.

```python
import jax
import jax.numpy as jnp
from jax import lax

NG = 10240
NGRID = 64
NB = 6
P_DEV = 4
PAIRS = 256
NBANDS = 384
NG_BLK = 1280
YS = 8


def draw_g_map(key, part):
    blocks = NG // NG_BLK
    slab_size = NGRID * YS * NGRID

    def one_block(block_number):
        block_key = jax.random.fold_in(jax.random.fold_in(key, 11), block_number)
        interior = jax.random.permutation(block_key, slab_size - 2)[:NG_BLK - 2].astype(jnp.int32) + 1
        chosen = jnp.concatenate([jnp.array([0, slab_size - 1], jnp.int32), interior])
        shuffle = jax.random.permutation(jax.random.fold_in(block_key, 3), NG_BLK)
        chosen = chosen[shuffle]
        x_index = chosen // (YS * NGRID)
        y_index = chosen // NGRID % YS + block_number * YS
        z_index = chosen % NGRID
        return (x_index * NGRID * NGRID + y_index * NGRID + z_index).astype(jnp.int32)
    return jax.vmap(one_block)(jnp.arange(blocks, dtype=jnp.int32)).reshape(NG)


def plant(values, own_key, smallest, high):
    longest = values.shape.index(max(values.shape))
    spots = []
    for shift in (0, 1):
        where = [jax.random.randint(jax.random.fold_in(own_key, axis), (), 0, length) for axis, length in enumerate(values.shape)]
        where[longest] = (where[longest] + shift) % values.shape[longest]
        spots.append(tuple(where))
    return values.at[spots[0]].set(smallest).at[spots[1]].set(high)


def block_scale(rng, dims, split, smallest, top_value):
    gain = 1.0
    for dim, blocks in split:
        steps = jax.random.uniform(jax.random.fold_in(jax.random.fold_in(rng, 6), dim), (blocks,), jnp.float32, smallest / len(split), top_value / len(split))
        gain = gain * jnp.repeat(jnp.exp(steps), dims[dim] // blocks).reshape((-1,) + (1,) * (len(dims) - 1 - dim))
    return gain


def normal_values(key, extent, spread, most, split=(), kind=jnp.bfloat16):
    result = spread * jax.random.normal(key, extent, jnp.float32)
    if split:
        result = result * block_scale(key, extent, split, -0.22, 0.18)
    return jnp.clip(result, -most, most).astype(kind)


def setup_inputs(seed: int = 0) -> dict:
    seeds = jax.random.split(jax.random.key(seed), 7)
    psi_val = normal_values(seeds[0], (NBANDS, NGRID, NGRID, 2 * NGRID), 0.7071, 6.0, ((0, 64), (1, 8)))
    psi_cond = normal_values(seeds[1], (NBANDS, NGRID, NGRID, 2 * NGRID), 0.7071, 6.0, ((0, 64), (1, 8)))
    pair_bands = plant(jax.random.randint(seeds[2], (PAIRS, 2), 0, NB), jax.random.fold_in(seeds[2], 1), 0, NB - 1).astype(jnp.int32)
    eps_val = jnp.clip(-4.125 + 4.0 * jax.random.uniform(seeds[3], (NBANDS,), jnp.float32) ** block_scale(seeds[3], (NBANDS,), ((0, 64),), -0.2, 0.2), -4.125, -0.125)
    eps_cond = jnp.clip(0.125 + 4.0 * jax.random.uniform(seeds[4], (NBANDS,), jnp.float32) ** block_scale(seeds[4], (NBANDS,), ((0, 64),), -0.2, 0.2), 0.125, 4.125)
    g_map = draw_g_map(jax.random.fold_in(seeds[6], 71), 0)
    return {"psi_val": psi_val, "psi_cond": psi_cond, "pair_bands": pair_bands, "eps_val": eps_val, "eps_cond": eps_cond, "g_map": g_map}


def reference(psi_val, psi_cond, pair_bands, eps_val, eps_cond, g_map):
    groups = NBANDS // NB
    valence_all = psi_val.reshape(groups, NB, NGRID, NGRID, 2 * NGRID)
    conduction_all = psi_cond.reshape(groups, NB, NGRID, NGRID, 2 * NGRID)
    pairs_all = pair_bands.reshape(groups, P_DEV, 2)
    valence_levels = eps_val.reshape(groups, NB)
    conduction_levels = eps_cond.reshape(groups, NB)

    def one_group(inputs):
        valence_bands, conduction_bands, band_pairs, valence_energy, conduction_energy = inputs
        valence_field = jnp.take(valence_bands, band_pairs[:, 0], axis=0).astype(jnp.float32)
        conduction_field = jnp.take(conduction_bands, band_pairs[:, 1], axis=0).astype(jnp.float32)
        valence_re = valence_field[..., :NGRID]
        valence_im = valence_field[..., NGRID:]
        conduction_re = conduction_field[..., :NGRID]
        conduction_im = conduction_field[..., NGRID:]
        density_re = valence_re * conduction_re + valence_im * conduction_im
        density_im = valence_re * conduction_im - valence_im * conduction_re
        spectrum = jnp.fft.fftn(lax.complex(density_re, density_im), axes=(1, 2, 3), norm="ortho")
        flattened = spectrum.reshape(P_DEV, NGRID * NGRID * NGRID)
        picked = jnp.take(flattened, g_map, axis=1)
        elements = jnp.stack([jnp.real(picked), jnp.imag(picked)], axis=1).astype(jnp.bfloat16)
        weights = 2.0 / (jnp.take(valence_energy, band_pairs[:, 0]) - jnp.take(conduction_energy, band_pairs[:, 1]))
        return elements, weights

    elements, weights = lax.map(one_group, (valence_all, conduction_all, pairs_all, valence_levels, conduction_levels))
    elements = elements.reshape(PAIRS, 2, NG)
    weights = weights.reshape(PAIRS)
    scaled = (weights[:, None, None] * elements.astype(jnp.float32)).astype(jnp.bfloat16)
    turned = jnp.stack([-scaled[:, 1], scaled[:, 0]], axis=1)
    right_side = elements.reshape(2 * PAIRS, NG)
    response_re = jnp.dot(scaled.reshape(2 * PAIRS, NG).T, right_side, preferred_element_type=jnp.float32)
    response_im = jnp.dot(turned.reshape(2 * PAIRS, NG).T, right_side, preferred_element_type=jnp.float32)
    return jnp.stack([response_re, response_im]) * (1.0 / PAIRS)
```

```python
import math

import jax
import jax.numpy as jnp
import numpy as np
from jax import lax
from jax.experimental import pallas as pl
from jax.experimental.pallas import tpu as pltpu
from jax.sharding import Mesh
from jax.sharding import PartitionSpec as P

N = 64
G_BLK = 1280
PAIRS = 256
ROWS = 160
MSG = 1664
F32 = jnp.float32
BF16 = jnp.bfloat16


def host_tables():
    k = np.arange(N)
    angle = 2.0 * math.pi * ((k[:, None] * k[None, :]) % N) / N
    c, s = np.cos(angle), np.sin(angle)
    top = np.concatenate([c, -s, -s, -c], axis=1)
    low = np.concatenate([s, c, c, -s], axis=1)
    z_table = np.concatenate([top, top, low, -low], axis=0)
    order = np.concatenate([k[0::2], k[1::2]])
    y_table = np.concatenate([c, s], axis=1)[order]
    to_re = np.stack([c, s], axis=1).reshape(2 * N, N)
    to_im = np.stack([-s, c], axis=1).reshape(2 * N, N)
    x_table = np.concatenate([to_re, to_im], axis=0)
    return z_table, y_table, x_table


def two_parts(table, axis):
    kind = np.dtype(BF16)
    high = table.astype(kind)
    return np.concatenate([high, (table - high.astype(np.float64)).astype(kind)], axis=axis)


def local_dft_kernel(bands, val, cond, z_tab, y_tab, out, scratch):
    del bands
    v = val[0].astype(F32).reshape(8 * N, 2 * N)
    c = cond[0].astype(F32).reshape(8 * N, 2 * N)
    products = jnp.concatenate([v * c, v * pltpu.roll(c, N, 1)], axis=1).astype(BF16)
    both = jnp.dot(products, z_tab[...], preferred_element_type=F32)
    along_z = (both[:, : 4 * N] + both[:, 4 * N :]).astype(BF16)
    parts = []
    for x in range(8):
        rows = along_z[x * N : (x + 1) * N]
        parts.append(jnp.concatenate([rows[:, : 2 * N], rows[:, 2 * N :]] * 2, axis=0))
    along_y = jnp.dot(y_tab[...], jnp.concatenate(parts, axis=1), preferred_element_type=F32)
    first = lax.broadcasted_iota(jnp.int32, (N // 2, 2 * N), 1) < N
    for x in range(8):
        tile = along_y[:, x * 2 * N : (x + 1) * 2 * N]
        even, odd = tile[: N // 2], tile[N // 2 :]
        scratch[pl.ds(x * N, N // 2), :] = jnp.where(first, even, pltpu.roll(odd, N, 1))
        scratch[pl.ds(x * N + N // 2, N // 2), :] = jnp.where(first, pltpu.roll(even, N, 1), odd)
    for k in range(N // 2):
        out[k // 4, k % 4] = scratch[pl.ds(k, 16, stride=N // 2), :].astype(BF16)


def local_dft(pair_bands, psi_val, psi_cond, z_tab, y_tab):
    band = lambda which: pl.BlockSpec((1, 8, N, 2 * N), lambda i, b: (b[i, which], 0, 0, 0))
    whole = lambda shape: pl.BlockSpec(shape, lambda i, b: (0, 0))
    return pl.pallas_call(
        local_dft_kernel,
        grid_spec=pltpu.PrefetchScalarGridSpec(
            num_scalar_prefetch=1,
            grid=(4,),
            in_specs=[band(0), band(1), whole(z_tab.shape), whole(y_tab.shape)],
            out_specs=pl.BlockSpec((8, 4, 16, 2 * N), lambda i, b: (0, 0, i, 0)),
            scratch_shapes=[pltpu.VMEM((8 * N, 2 * N), F32)],
        ),
        out_shape=jax.ShapeDtypeStruct((8, 4, N, 2 * N), BF16),
        name="local_dft",
    )(pair_bands, psi_val, psi_cond, z_tab, y_tab)


def picks_kernel(g_map, x_tab, column_pick, twiddle):
    g = g_map[...]
    row = lax.broadcasted_iota(jnp.int32, (8 * N, G_BLK), 0)
    column_pick[...] = jnp.where(row == (g & (8 * N - 1)), 1.0, 0.0).astype(BF16)
    row = lax.broadcasted_iota(jnp.int32, (2 * N, G_BLK), 0)
    x_pick = jnp.where((row & (N - 1)) == (g >> 12), 1.0, 0.0).astype(BF16)
    twiddle[...] = jnp.dot(x_tab[...], x_pick, preferred_element_type=F32)


def picks(g_map, x_tab):
    return pl.pallas_call(
        picks_kernel,
        out_shape=(
            jax.ShapeDtypeStruct((8 * N, G_BLK), BF16),
            jax.ShapeDtypeStruct((4 * N, G_BLK), F32),
        ),
        name="picks",
    )(g_map, x_tab)


def elements_kernel(bands, e_val, e_cond, slabs, column_pick, twiddle, elements, scaled):
    step = 256
    row = lax.broadcasted_iota(jnp.int32, (8, step), 0) % 4
    gap = jnp.zeros((8, step), F32)
    for i in range(4):
        gap = jnp.where(row == i, e_val[bands[i, 0]] - e_cond[bands[i, 1]], gap)
    weight = 2.0 / gap
    left = jnp.concatenate([slabs[:, s].reshape(8 * N, 2 * N) for s in range(4)], axis=1)
    for n in range(G_BLK // step):
        cols = pl.ds(n * step, step)
        picked = jnp.dot(left, column_pick[:, cols], preferred_element_type=F32)
        picked = picked.reshape(8, 4, 16, step)
        halves = []
        for h in range(2):
            factor = twiddle[pl.ds(h * 2 * N, 2 * N), cols].reshape(8, 1, 16, step)
            halves.append(jnp.sum(jnp.sum(picked * factor, axis=0), axis=1))
        values = (jnp.concatenate(halves, axis=0) * (1.0 / (N * 8))).astype(BF16)
        elements[:, cols] = values
        weighted = (weight * values.astype(F32)).astype(BF16)
        for f in range(8):
            scaled[f, :, cols] = weighted


def make_elements(pair_bands, eps_val, eps_cond, slabs, column_pick, twiddle):
    smem = pl.BlockSpec(memory_space=pltpu.SMEM)
    vmem = pl.BlockSpec(memory_space=pltpu.VMEM)
    return pl.pallas_call(
        elements_kernel,
        in_specs=[smem] * 3 + [vmem] * 3,
        out_shape=(
            jax.ShapeDtypeStruct((8, G_BLK), BF16),
            jax.ShapeDtypeStruct((8, 8, G_BLK), BF16),
        ),
        name="elements",
    )(pair_bands, eps_val, eps_cond, slabs, column_pick, twiddle)


def messages_kernel(core, elements, scaled, out):
    swapped = core[0] == 1
    values = elements[...]
    pad = jnp.zeros((8, MSG - G_BLK - 2 * ROWS), F32)
    for j in range(32):
        out[j, :, pl.ds(0, G_BLK)] = values
        part = (j % 4) * 2 * ROWS
        rows = scaled[j // 4].astype(F32)[:, part : part + 2 * ROWS]
        first, second = rows[:, :ROWS], rows[:, ROWS:]
        mine = jnp.where(swapped, second, first)
        other = jnp.where(swapped, first, second)
        out[j, :, pl.ds(G_BLK, MSG - G_BLK)] = jnp.concatenate([mine, pad, other], axis=1).astype(BF16)


def make_messages(core, elements, scaled):
    smem = pl.BlockSpec(memory_space=pltpu.SMEM)
    vmem = pl.BlockSpec(memory_space=pltpu.VMEM)
    return pl.pallas_call(
        messages_kernel,
        in_specs=[smem, vmem, vmem],
        out_shape=jax.ShapeDtypeStruct((32, 8, MSG), BF16),
        name="messages",
    )(core, elements, scaled)


def product_kernel(mine_rows, other_rows, mine_cols, other_cols, out, left):
    @pl.when(pl.program_id(0) == 0)
    def _():
        shift = MSG - G_BLK - ROWS
        a = mine_rows[...].astype(F32)
        b = pltpu.roll(other_rows[...].astype(F32), MSG - G_BLK - shift, 1)
        rows = jnp.concatenate([a[:, :256], b[:, :256]], axis=0)
        turned = pltpu.roll(rows.reshape(64, 8, 256), 4, 1)
        sign = jnp.where(lax.broadcasted_iota(jnp.int32, (64, 8, 256), 1) < 4, -1.0, 1.0)
        turned = (turned * sign).reshape(512, 256)
        left[pl.ds(0, ROWS), :] = rows.T[:ROWS].astype(BF16)
        left[pl.ds(ROWS, ROWS), :] = turned.T[:ROWS].astype(BF16)

    right = jnp.concatenate([mine_cols[...], other_cols[...]], axis=0)
    result = jnp.dot(left[...], right, preferred_element_type=F32) * (1.0 / PAIRS)
    out[0] = result[:ROWS]
    out[1] = result[ROWS:]


def product(mine, other):
    step = 256
    tail = MSG - G_BLK
    mine, other = mine.reshape(256, MSG), other.reshape(256, MSG)
    rows_m, rows_o = mine[:, G_BLK:], other[:, G_BLK:]
    cols = pl.BlockSpec((256, step), lambda n: (0, n))
    rows = pl.BlockSpec((256, tail), lambda n: (0, 0))
    return pl.pallas_call(
        product_kernel,
        grid=(G_BLK // step,),
        in_specs=[rows, rows, cols, cols],
        out_specs=pl.BlockSpec((2, ROWS, step), lambda n: (0, 0, n)),
        out_shape=jax.ShapeDtypeStruct((2, ROWS, G_BLK), F32),
        scratch_shapes=[pltpu.VMEM((2 * ROWS, 512), BF16)],
        name="product",
    )(rows_m, rows_o, mine, other)


def on_device(psi_val, psi_cond, pair_bands, eps_val, eps_cond, g_map):
    z_table, y_table, x_table = host_tables()
    z_tab = jnp.asarray(two_parts(z_table, 1))
    y_tab = jnp.asarray(two_parts(y_table, 1))
    x_tab = jnp.asarray(two_parts(x_table, 1))
    slabs = local_dft(pair_bands, psi_val, psi_cond, z_tab, y_tab)
    slabs = lax.all_to_all(slabs, ("x", "zl"), 0, 0, tiled=True)
    column_pick, twiddle = picks(g_map.reshape(1, G_BLK), x_tab)
    elements, scaled = make_elements(pair_bands, eps_val, eps_cond, slabs, column_pick, twiddle)
    scaled = lax.all_to_all(scaled, ("x", "zl"), 0, 0, tiled=True)
    core = lax.axis_index("core").astype(jnp.int32).reshape(1)
    mine = lax.all_to_all(make_messages(core, elements, scaled), ("zh", "y"), 0, 0, tiled=True)
    other = lax.ppermute(mine, "core", [(0, 1), (1, 0)])
    return product(mine, other)


def solution(mesh):
    fine = Mesh(mesh.devices.reshape(4, 8, 2, 4, 2), ("zh", "y", "core", "x", "zl"))
    pair, fft = ("zh", "y", "core"), ("x", "zl")
    in_specs = (
        P(pair, fft, None, None),
        P(pair, fft, None, None),
        P(pair, None),
        P(pair),
        P(pair),
        P(fft),
    )
    return jax.shard_map(
        on_device, mesh=fine, in_specs=in_specs, out_specs=P(None, pair, fft), check_vma=False
    )
```

```python
import math

import jax
import jax.numpy as jnp
import numpy as np
from jax import lax
from jax.experimental import pallas as pl
from jax.experimental.pallas import tpu as pltpu
from jax.sharding import Mesh
from jax.sharding import PartitionSpec as P

N = 64
G_BLK = 1280
PAIRS = 256
ROWS = 160
MSG = 1664
F32 = jnp.float32
BF16 = jnp.bfloat16


def host_tables():
    k = np.arange(N)
    angle = 2.0 * math.pi * ((k[:, None] * k[None, :]) % N) / N
    c, s = np.cos(angle), np.sin(angle)
    top = np.concatenate([c, -s, -s, -c], axis=1)
    low = np.concatenate([s, c, c, -s], axis=1)
    z_table = np.concatenate([top, top, low, -low], axis=0)
    order = np.concatenate([k[0::2], k[1::2]])
    y_table = np.concatenate([c, s], axis=1)[order]
    to_re = np.stack([c, s], axis=1).reshape(2 * N, N)
    to_im = np.stack([-s, c], axis=1).reshape(2 * N, N)
    x_table = np.concatenate([to_re, to_im], axis=0)
    return z_table, y_table, x_table


def two_parts(table, axis):
    kind = np.dtype(BF16)
    high = table.astype(kind)
    return np.concatenate([high, (table - high.astype(np.float64)).astype(kind)], axis=axis)


def in_vmem(*arrays):
    return [pltpu.with_memory_space_constraint(a, pltpu.VMEM) for a in arrays]


def limit(mib):
    return pltpu.CompilerParams(vmem_limit_bytes=mib << 20)


SMEM = pl.BlockSpec(memory_space=pltpu.SMEM)
VMEM = pl.BlockSpec(memory_space=pltpu.VMEM)
ANY = pl.BlockSpec(memory_space=pl.ANY)


def local_dft_kernel(bands, val, cond, z_tab, y_tab, out, scratch):
    first = lax.broadcasted_iota(jnp.int32, (N // 2, 2 * N), 1) < N

    def along_z(i):
        v = val[bands[0, i]].astype(F32).reshape(8 * N, 2 * N)
        c = cond[bands[1, i]].astype(F32).reshape(8 * N, 2 * N)
        products = jnp.concatenate([v * c, v * pltpu.roll(c, N, 1)], axis=1).astype(BF16)
        both = jnp.dot(products, z_tab[...], preferred_element_type=F32)
        return both.astype(BF16)

    def along_y(i, mid):
        parts = []
        for x in range(8):
            rows = mid[x * N : (x + 1) * N]
            parts.append(jnp.concatenate([rows[:, : 2 * N], rows[:, 2 * N :]], axis=0))
        res = jnp.dot(y_tab[...], jnp.concatenate(parts, axis=1), preferred_element_type=F32)
        base = i * 8 * N
        for x in range(8):
            tile = res[:, x * 2 * N : (x + 1) * 2 * N]
            even, odd = tile[: N // 2], tile[N // 2 :]
            scratch[pl.ds(base + x * N, N // 2), :] = jnp.where(first, even, pltpu.roll(odd, N, 1))
            scratch[pl.ds(base + x * N + N // 2, N // 2), :] = jnp.where(first, pltpu.roll(even, N, 1), odd)

    def store(i):
        base = i * 8 * N
        for k in range(N // 2):
            rows = scratch[pl.ds(base + k, 16, stride=N // 2), :]
            out[k // 4, k % 4, pl.ds(16 * i, 16), :] = rows.astype(BF16)

    mids = [along_z(0)]
    for i in range(4):
        if i < 3:
            mids.append(along_z(i + 1))
        along_y(i, mids[i])
        store(i)


def local_dft(bands, psi_val, psi_cond, z_tab, y_tab):
    return pl.pallas_call(
        local_dft_kernel,
        in_specs=[SMEM, VMEM, VMEM, VMEM, VMEM],
        out_specs=VMEM,
        out_shape=pltpu.VMEM((8, 4, N, 2 * N), BF16),
        scratch_shapes=[pltpu.VMEM((4 * 8 * N, 2 * N), F32)],
        name="local_dft",
    )(bands, psi_val, psi_cond, z_tab, y_tab)


def picks_kernel(g_map, x_tab, column_pick, twiddle):
    g = g_map[...]
    row = lax.broadcasted_iota(jnp.int32, (8 * N, G_BLK), 0)
    column_pick[...] = jnp.where(row == (g & (8 * N - 1)), 1.0, 0.0).astype(BF16)
    row = lax.broadcasted_iota(jnp.int32, (2 * N, G_BLK), 0)
    x_pick = jnp.where((row & (N - 1)) == (g >> 12), 1.0, 0.0).astype(BF16)
    twiddle[...] = jnp.dot(x_tab[...], x_pick, preferred_element_type=F32)


def picks(g_map, x_tab):
    return pl.pallas_call(
        picks_kernel,
        in_specs=[VMEM, VMEM],
        out_specs=(VMEM, VMEM),
        out_shape=(pltpu.VMEM((8 * N, G_BLK), BF16), pltpu.VMEM((4 * N, G_BLK), F32)),
        compiler_params=limit(8),
        name="picks",
    )(g_map, x_tab)


def elements_kernel(bands, e_val, e_cond, slabs, column_pick, twiddle, elements, scaled):
    step = 256
    row = lax.broadcasted_iota(jnp.int32, (8, step), 0) % 4
    gap = jnp.zeros((8, step), F32)
    for i in range(4):
        gap = jnp.where(row == i, e_val[bands[0, i]] - e_cond[bands[1, i]], gap)
    weight = 2.0 / gap
    left = jnp.concatenate([slabs[:, s].reshape(8 * N, 2 * N) for s in range(4)], axis=1)
    for n in range(G_BLK // step):
        cols = pl.ds(n * step, step)
        picked = jnp.dot(left, column_pick[:, cols], preferred_element_type=F32)
        picked = picked.reshape(8, 4, 16, step)
        halves = []
        for h in range(2):
            factor = twiddle[pl.ds(h * 2 * N, 2 * N), cols].reshape(8, 1, 16, step)
            halves.append(jnp.sum(jnp.sum(picked * factor, axis=0), axis=1))
        values = (jnp.concatenate(halves, axis=0) * (1.0 / (N * 8))).astype(BF16)
        elements[:, cols] = values
        weighted = (weight * values.astype(F32)).astype(BF16)
        for f in range(8):
            scaled[f, :, cols] = weighted


def make_elements(bands, eps_val, eps_cond, slabs, column_pick, twiddle):
    return pl.pallas_call(
        elements_kernel,
        in_specs=[SMEM] * 3 + [VMEM] * 3,
        out_specs=(VMEM, VMEM),
        out_shape=(pltpu.VMEM((8, G_BLK), BF16), pltpu.VMEM((8, 8, G_BLK), BF16)),
        compiler_params=limit(12),
        name="elements",
    )(bands, eps_val, eps_cond, *in_vmem(slabs, column_pick, twiddle))


def messages_kernel(core, elements, scaled, out):
    swapped = core[0] == 1
    values = elements[...]
    pad = jnp.zeros((8, MSG - G_BLK - 2 * ROWS), F32)
    for j in range(32):
        out[j, :, pl.ds(0, G_BLK)] = values
        part = (j % 4) * 2 * ROWS
        rows = scaled[j // 4].astype(F32)[:, part : part + 2 * ROWS]
        first, second = rows[:, :ROWS], rows[:, ROWS:]
        mine = jnp.where(swapped, second, first)
        other = jnp.where(swapped, first, second)
        tail = jnp.concatenate([mine, pad, other], axis=1).astype(BF16)
        out[j, :, pl.ds(G_BLK, MSG - G_BLK)] = tail


def make_messages(core, elements, scaled):
    return pl.pallas_call(
        messages_kernel,
        in_specs=[SMEM, VMEM, VMEM],
        out_specs=VMEM,
        out_shape=pltpu.VMEM((32, 8, MSG), BF16),
        compiler_params=limit(4),
        name="messages",
    )(core, *in_vmem(elements, scaled))


def left_side(tail, skip):
    rows = tail.astype(F32)
    turned = pltpu.roll(rows.reshape(32, 8, 256), 4, 1)
    sign = jnp.where(lax.broadcasted_iota(jnp.int32, (32, 8, 256), 1) < 4, -1.0, 1.0)
    turned = (turned * sign).reshape(256, 256)
    keep = slice(skip, skip + ROWS)
    return jnp.concatenate([rows.T[keep].astype(BF16), turned.T[keep].astype(BF16)], axis=0)


def first_half_kernel(data, out):
    left = left_side(data[:, pl.ds(G_BLK, 256)], 0)
    for n in range(5):
        cols = pl.ds(n * 256, 256)
        out[:, cols] = jnp.dot(left, data[:, cols], preferred_element_type=F32)


def first_half(data):
    return pl.pallas_call(
        first_half_kernel,
        in_specs=[VMEM],
        out_specs=VMEM,
        out_shape=pltpu.VMEM((2 * ROWS, G_BLK), F32),
        compiler_params=limit(8),
        name="first_half",
    )(*in_vmem(data.reshape(256, MSG)))


def second_half_kernel(data, start, out, stage, sems):
    left = left_side(data[:, pl.ds(G_BLK + 128, 256)], 96)
    copies = []
    for n in range(5):
        cols = pl.ds(n * 256, 256)
        total = start[:, cols] + jnp.dot(left, data[:, cols], preferred_element_type=F32)
        total = total * (1.0 / PAIRS)
        stage[0, :, cols] = total[:ROWS]
        stage[1, :, cols] = total[ROWS:]
        copy = pltpu.make_async_copy(stage.at[:, :, cols], out.at[:, :, cols], sems.at[n])
        copy.start()
        copies.append(copy)
    for copy in copies:
        copy.wait()


def second_half(data, start):
    return pl.pallas_call(
        second_half_kernel,
        in_specs=[VMEM, VMEM],
        out_specs=ANY,
        out_shape=jax.ShapeDtypeStruct((2, ROWS, G_BLK), F32),
        scratch_shapes=[pltpu.VMEM((2, ROWS, G_BLK), F32), pltpu.SemaphoreType.DMA((5,))],
        compiler_params=limit(8),
        name="second_half",
    )(*in_vmem(data.reshape(256, MSG), start))


def on_device(psi_val, psi_cond, pair_bands, eps_val, eps_cond, g_map):
    z_table, y_table, x_table = host_tables()
    z_tab = jnp.asarray(z_table.astype(np.dtype(BF16)))
    y_tab = jnp.asarray(y_table.astype(np.dtype(BF16)))
    x_tab = jnp.asarray(two_parts(x_table, 1))
    bands = pair_bands.T
    slabs = local_dft(bands, psi_val, psi_cond, z_tab, y_tab)
    slabs = lax.all_to_all(slabs, ("x", "zl"), 0, 0, tiled=True)
    column_pick, twiddle = picks(g_map.reshape(1, G_BLK), x_tab)
    elements, scaled = make_elements(bands, eps_val, eps_cond, slabs, column_pick, twiddle)
    scaled = lax.all_to_all(scaled, ("x", "zl"), 0, 0, tiled=True)
    core = lax.axis_index("core").astype(jnp.int32).reshape(1)
    data = make_messages(core, elements, scaled)
    mine = lax.all_to_all(data, ("zh", "y"), 0, 0, tiled=True)
    other = lax.ppermute(mine, "core", [(0, 1), (1, 0)])
    return second_half(other, first_half(mine))


def solution(mesh):
    fine = Mesh(mesh.devices.reshape(4, 8, 2, 4, 2), ("zh", "y", "core", "x", "zl"))
    pair, fft = ("zh", "y", "core"), ("x", "zl")
    in_specs = (
        P(pair, fft, None, None),
        P(pair, fft, None, None),
        P(pair, None),
        P(pair),
        P(pair),
        P(fft),
    )
    return jax.shard_map(
        on_device, mesh=fine, in_specs=in_specs, out_specs=P(None, pair, fft), check_vma=False
    )
```

```python
import math

import jax
import jax.numpy as jnp
import numpy as np
from jax import lax
from jax.experimental import pallas as pl
from jax.experimental.pallas import tpu as pltpu
from jax.sharding import Mesh
from jax.sharding import PartitionSpec as P

N = 64
G_BLK = 1280
PAIRS = 256
ROWS = 160
MSG = 1664
F32 = jnp.float32
BF16 = jnp.bfloat16


def host_tables():
    k = np.arange(N)
    angle = 2.0 * math.pi * ((k[:, None] * k[None, :]) % N) / N
    c, s = np.cos(angle), np.sin(angle)
    top = np.concatenate([c, -s, -s, -c], axis=1)
    low = np.concatenate([s, c, c, -s], axis=1)
    z_table = np.concatenate([top, top, low, -low], axis=0)
    order = np.concatenate([k[0::2], k[1::2]])
    y_table = np.concatenate([c, s], axis=1)[order]
    to_re = np.stack([c, s], axis=1).reshape(2 * N, N)
    to_im = np.stack([-s, c], axis=1).reshape(2 * N, N)
    x_table = np.concatenate([to_re, to_im], axis=0)
    return z_table, y_table, x_table


def two_parts(table, axis):
    kind = np.dtype(BF16)
    high = table.astype(kind)
    return np.concatenate([high, (table - high.astype(np.float64)).astype(kind)], axis=axis)


def in_vmem(*arrays):
    return [pltpu.with_memory_space_constraint(a, pltpu.VMEM) for a in arrays]


def limit(mib):
    return pltpu.CompilerParams(vmem_limit_bytes=mib << 20)


SMEM = pl.BlockSpec(memory_space=pltpu.SMEM)
VMEM = pl.BlockSpec(memory_space=pltpu.VMEM)
ANY = pl.BlockSpec(memory_space=pl.ANY)


def local_dft_kernel(bands, val, cond, z_tab, y_tab, out, scratch):
    first = lax.broadcasted_iota(jnp.int32, (N // 2, 2 * N), 1) < N

    def along_z(i):
        v = val[bands[0, i]].reshape(8 * N, 2 * N)
        c = cond[bands[1, i]].reshape(8 * N, 2 * N)
        crossed = jnp.concatenate([c[:, N:], c[:, :N]], axis=1)
        products = jnp.concatenate([v * c, v * crossed], axis=1)
        both = jnp.dot(products, z_tab[...], preferred_element_type=F32)
        return both.astype(BF16)

    def along_y(i, mid):
        parts = []
        for x in range(8):
            rows = mid[x * N : (x + 1) * N]
            parts.append(jnp.concatenate([rows[:, : 2 * N], rows[:, 2 * N :]], axis=0))
        res = jnp.dot(y_tab[...], jnp.concatenate(parts, axis=1), preferred_element_type=F32)
        base = i * 8 * N
        for x in range(8):
            tile = res[:, x * 2 * N : (x + 1) * 2 * N]
            even, odd = tile[: N // 2], tile[N // 2 :]
            scratch[pl.ds(base + x * N, N // 2), :] = jnp.where(first, even, pltpu.roll(odd, N, 1))
            scratch[pl.ds(base + x * N + N // 2, N // 2), :] = jnp.where(first, pltpu.roll(even, N, 1), odd)

    def store(i):
        base = i * 8 * N
        for k in range(N // 2):
            rows = scratch[pl.ds(base + k, 16, stride=N // 2), :]
            out[k // 4, k % 4, pl.ds(16 * i, 16), :] = rows.astype(BF16)

    mids = [along_z(0)]
    for i in range(4):
        if i < 3:
            mids.append(along_z(i + 1))
        along_y(i, mids[i])
        store(i)


def local_dft(bands, psi_val, psi_cond, z_tab, y_tab):
    return pl.pallas_call(
        local_dft_kernel,
        in_specs=[SMEM, VMEM, VMEM, VMEM, VMEM],
        out_specs=VMEM,
        out_shape=pltpu.VMEM((8, 4, N, 2 * N), BF16),
        scratch_shapes=[pltpu.VMEM((4 * 8 * N, 2 * N), F32)],
        name="local_dft",
    )(bands, psi_val, psi_cond, z_tab, y_tab)


def picks_kernel(bands, e_val, e_cond, g_map, x_tab, column_pick, twiddle, weight):
    row = lax.broadcasted_iota(jnp.int32, (8, 256), 0) % 4
    gap = jnp.zeros((8, 256), F32)
    for i in range(4):
        gap = jnp.where(row == i, e_val[bands[0, i]] - e_cond[bands[1, i]], gap)
    weight[...] = 2.0 / gap
    g = g_map[...]
    row = lax.broadcasted_iota(jnp.int32, (8 * N, G_BLK), 0)
    column_pick[...] = jnp.where(row == (g & (8 * N - 1)), 1.0, 0.0).astype(BF16)
    row = lax.broadcasted_iota(jnp.int32, (2 * N, G_BLK), 0)
    x_pick = jnp.where((row & (N - 1)) == (g >> 12), 1.0, 0.0).astype(BF16)
    twiddle[...] = jnp.dot(x_tab[...], x_pick, preferred_element_type=F32)


def picks(bands, eps_val, eps_cond, g_map, x_tab):
    return pl.pallas_call(
        picks_kernel,
        in_specs=[SMEM] * 3 + [VMEM] * 2,
        out_specs=(VMEM,) * 3,
        out_shape=(
            pltpu.VMEM((8 * N, G_BLK), BF16),
            pltpu.VMEM((4 * N, G_BLK), F32),
            pltpu.VMEM((8, 256), F32),
        ),
        compiler_params=limit(8),
        name="picks",
    )(bands, eps_val, eps_cond, g_map, x_tab)


def elements_kernel(slabs, column_pick, twiddle, weight, elements, scaled):
    step = 256
    left = jnp.concatenate([slabs[:, s].reshape(8 * N, 2 * N) for s in range(4)], axis=1)
    for n in range(G_BLK // step):
        cols = pl.ds(n * step, step)
        picked = jnp.dot(left, column_pick[:, cols], preferred_element_type=F32)
        picked = picked.reshape(8, 4, 16, step)
        halves = []
        for h in range(2):
            factor = twiddle[pl.ds(h * 2 * N, 2 * N), cols].reshape(8, 1, 16, step)
            halves.append(jnp.sum(jnp.sum(picked * factor, axis=0), axis=1))
        values = (jnp.concatenate(halves, axis=0) * (1.0 / (N * 8))).astype(BF16)
        elements[:, cols] = values
        weighted = (weight[...] * values.astype(F32)).astype(BF16)
        for f in range(8):
            scaled[f, :, cols] = weighted


def make_elements(slabs, column_pick, twiddle, weight):
    return pl.pallas_call(
        elements_kernel,
        in_specs=[VMEM] * 4,
        out_specs=(VMEM, VMEM),
        out_shape=(pltpu.VMEM((8, G_BLK), BF16), pltpu.VMEM((8, 8, G_BLK), BF16)),
        compiler_params=limit(12),
        name="elements",
    )(*in_vmem(slabs, column_pick, twiddle, weight))


def messages_kernel(elements, scaled, out):
    swapped = lax.axis_index("core") == 1
    values = elements[...]
    pad = jnp.zeros((8, MSG - G_BLK - 2 * ROWS), F32)
    for j in range(32):
        out[j, :, pl.ds(0, G_BLK)] = values
        part = (j % 4) * 2 * ROWS
        rows = scaled[j // 4].astype(F32)[:, part : part + 2 * ROWS]
        first, second = rows[:, :ROWS], rows[:, ROWS:]
        mine = jnp.where(swapped, second, first)
        other = jnp.where(swapped, first, second)
        tail = jnp.concatenate([mine, pad, other], axis=1).astype(BF16)
        out[j, :, pl.ds(G_BLK, MSG - G_BLK)] = tail


def make_messages(elements, scaled):
    return pl.pallas_call(
        messages_kernel,
        in_specs=[VMEM, VMEM],
        out_specs=VMEM,
        out_shape=pltpu.VMEM((32, 8, MSG), BF16),
        compiler_params=limit(4),
        name="messages",
    )(*in_vmem(elements, scaled))


def left_side(tail, skip):
    rows = tail.astype(F32)
    turned = pltpu.roll(rows.reshape(32, 8, 256), 4, 1)
    sign = jnp.where(lax.broadcasted_iota(jnp.int32, (32, 8, 256), 1) < 4, -1.0, 1.0)
    turned = (turned * sign).reshape(256, 256)
    keep = slice(skip, skip + ROWS)
    return jnp.concatenate([rows.T[keep].astype(BF16), turned.T[keep].astype(BF16)], axis=0)


def first_half_kernel(data, out):
    left = left_side(data[:, pl.ds(G_BLK, 256)], 0)
    for n in range(5):
        cols = pl.ds(n * 256, 256)
        out[:, cols] = jnp.dot(left, data[:, cols], preferred_element_type=F32)


def first_half(data):
    return pl.pallas_call(
        first_half_kernel,
        in_specs=[VMEM],
        out_specs=VMEM,
        out_shape=pltpu.VMEM((2 * ROWS, G_BLK), F32),
        compiler_params=limit(8),
        name="first_half",
    )(*in_vmem(data.reshape(256, MSG)))


def second_half_kernel(data, start, out, stage, sems):
    left = left_side(data[:, pl.ds(G_BLK + 128, 256)], 96)
    copies = []
    for n in range(5):
        cols = pl.ds(n * 256, 256)
        total = start[:, cols] + jnp.dot(left, data[:, cols], preferred_element_type=F32)
        total = total * (1.0 / PAIRS)
        stage[0, :, cols] = total[:ROWS]
        stage[1, :, cols] = total[ROWS:]
        copy = pltpu.make_async_copy(stage.at[:, :, cols], out.at[:, :, cols], sems.at[n])
        copy.start()
        copies.append(copy)
    for copy in copies:
        copy.wait()


def second_half(data, start):
    return pl.pallas_call(
        second_half_kernel,
        in_specs=[VMEM, VMEM],
        out_specs=ANY,
        out_shape=jax.ShapeDtypeStruct((2, ROWS, G_BLK), F32),
        scratch_shapes=[pltpu.VMEM((2, ROWS, G_BLK), F32), pltpu.SemaphoreType.DMA((5,))],
        compiler_params=limit(8),
        name="second_half",
    )(*in_vmem(data.reshape(256, MSG), start))


def on_device(psi_val, psi_cond, pair_bands, eps_val, eps_cond, g_map):
    z_table, y_table, x_table = host_tables()
    z_tab = jnp.asarray(z_table.astype(np.dtype(BF16)))
    y_tab = jnp.asarray(y_table.astype(np.dtype(BF16)))
    x_tab = jnp.asarray(two_parts(x_table, 1))
    bands = pair_bands.T
    slabs = local_dft(bands, psi_val, psi_cond, z_tab, y_tab)
    slabs = lax.all_to_all(slabs, ("x", "zl"), 0, 0, tiled=True)
    picked = picks(bands, eps_val, eps_cond, g_map.reshape(1, G_BLK), x_tab)
    elements, scaled = make_elements(slabs, *picked)
    scaled = lax.all_to_all(scaled, ("x", "zl"), 0, 0, tiled=True)
    data = make_messages(elements, scaled)
    mine = lax.all_to_all(data, ("zh", "y"), 0, 0, tiled=True)
    other = lax.ppermute(mine, "core", [(0, 1), (1, 0)])
    return second_half(other, first_half(mine))


def solution(mesh):
    fine = Mesh(mesh.devices.reshape(4, 8, 2, 4, 2), ("zh", "y", "core", "x", "zl"))
    pair, fft = ("zh", "y", "core"), ("x", "zl")
    in_specs = (
        P(pair, fft, None, None),
        P(pair, fft, None, None),
        P(pair, None),
        P(pair),
        P(pair),
        P(fft),
    )
    return jax.shard_map(
        on_device, mesh=fine, in_specs=in_specs, out_specs=P(None, pair, fft), check_vma=False
    )
```

```python
import math

import jax
import jax.numpy as jnp
import numpy as np
from jax import lax
from jax.experimental import pallas as pl
from jax.experimental.pallas import tpu as pltpu
from jax.sharding import Mesh
from jax.sharding import PartitionSpec as P


N = 64
G_BLK = 1280
PAIRS = 256
ROWS = 160
TAIL = 384
F32 = jnp.float32
BF16 = jnp.bfloat16


def host_tables():
    k = np.arange(N)
    angle = 2.0 * math.pi * ((k[:, None] * k[None, :]) % N) / N
    c, s = np.cos(angle), np.sin(angle)
    top = np.concatenate([c, -s, -s, -c], axis=1)
    low = np.concatenate([s, c, c, -s], axis=1)
    z_table = np.concatenate([top, top, low, -low], axis=0)
    order = np.concatenate([k[0::2], k[1::2]])
    y_table = np.concatenate([c, s], axis=1)[order]
    to_re = np.stack([c, s], axis=1).reshape(2 * N, N)
    to_im = np.stack([-s, c], axis=1).reshape(2 * N, N)
    x_table = np.concatenate([to_re, to_im], axis=0)
    return z_table, y_table, x_table


def two_parts(table, axis):
    kind = np.dtype(BF16)
    high = table.astype(kind)
    return np.concatenate([high, (table - high.astype(np.float64)).astype(kind)], axis=axis)


def in_vmem(*arrays):
    return [pltpu.with_memory_space_constraint(a, pltpu.VMEM) for a in arrays]


def limit(mib):
    return pltpu.CompilerParams(vmem_limit_bytes=mib << 20)


SMEM = pl.BlockSpec(memory_space=pltpu.SMEM)
VMEM = pl.BlockSpec(memory_space=pltpu.VMEM)
ANY = pl.BlockSpec(memory_space=pl.ANY)


def local_dft_kernel(bands, val, cond, z_tab, y_tab, out, scratch):
    first = lax.broadcasted_iota(jnp.int32, (N // 2, 2 * N), 1) < N

    def along_z(i):
        v = val[bands[0, i]].reshape(8 * N, 2 * N)
        c = cond[bands[1, i]].reshape(8 * N, 2 * N)
        crossed = jnp.concatenate([c[:, N:], c[:, :N]], axis=1)
        products = jnp.concatenate([v * c, v * crossed], axis=1)
        both = jnp.dot(products, z_tab[...], preferred_element_type=F32)
        return both.astype(BF16)

    def along_y(i, mid):
        parts = []
        for x in range(8):
            rows = mid[x * N : (x + 1) * N]
            parts.append(jnp.concatenate([rows[:, : 2 * N], rows[:, 2 * N :]], axis=0))
        res = jnp.dot(y_tab[...], jnp.concatenate(parts, axis=1), preferred_element_type=F32)
        base = i * 8 * N
        for x in range(8):
            tile = res[:, x * 2 * N : (x + 1) * 2 * N]
            even, odd = tile[: N // 2], tile[N // 2 :]
            scratch[pl.ds(base + x * N, N // 2), :] = jnp.where(first, even, pltpu.roll(odd, N, 1))
            scratch[pl.ds(base + x * N + N // 2, N // 2), :] = jnp.where(first, pltpu.roll(even, N, 1), odd)

    def store(i):
        base = i * 8 * N
        for k in range(N // 2):
            rows = scratch[pl.ds(base + k, 16, stride=N // 2), :]
            out[k // 4, k % 4, pl.ds(16 * i, 16), :] = rows.astype(BF16)

    mids = [along_z(0)]
    for i in range(4):
        if i < 3:
            mids.append(along_z(i + 1))
        along_y(i, mids[i])
        store(i)


def local_dft(bands, psi_val, psi_cond, z_tab, y_tab):
    return pl.pallas_call(
        local_dft_kernel,
        in_specs=[SMEM, VMEM, VMEM, VMEM, VMEM],
        out_specs=VMEM,
        out_shape=pltpu.VMEM((8, 4, N, 2 * N), BF16),
        scratch_shapes=[pltpu.VMEM((4 * 8 * N, 2 * N), F32)],
        name="local_dft",
    )(bands, psi_val, psi_cond, z_tab, y_tab)


def picks_kernel(bands, e_val, e_cond, g_map, x_tab, column_pick, twiddle, weight):
    row = lax.broadcasted_iota(jnp.int32, (8, 256), 0) % 4
    gap = jnp.zeros((8, 256), F32)
    for i in range(4):
        gap = jnp.where(row == i, e_val[bands[0, i]] - e_cond[bands[1, i]], gap)
    weight[...] = 2.0 / gap
    g = g_map[...]
    row = lax.broadcasted_iota(jnp.int32, (8 * N, G_BLK), 0)
    column_pick[...] = jnp.where(row == (g & (8 * N - 1)), 1.0, 0.0).astype(BF16)
    row = lax.broadcasted_iota(jnp.int32, (2 * N, G_BLK), 0)
    x_pick = jnp.where((row & (N - 1)) == (g >> 12), 1.0, 0.0).astype(BF16)
    twiddle[...] = jnp.dot(x_tab[...], x_pick, preferred_element_type=F32)


def picks(bands, eps_val, eps_cond, g_map, x_tab):
    return pl.pallas_call(
        picks_kernel,
        in_specs=[SMEM] * 3 + [VMEM] * 2,
        out_specs=(VMEM,) * 3,
        out_shape=(
            pltpu.VMEM((8 * N, G_BLK), BF16),
            pltpu.VMEM((4 * N, G_BLK), F32),
            pltpu.VMEM((8, 256), F32),
        ),
        compiler_params=limit(8),
        name="picks",
    )(bands, eps_val, eps_cond, g_map, x_tab)


def elements_kernel(slabs, column_pick, twiddle, weight, columns, *row_parts):
    step = 256
    left = jnp.concatenate([slabs[:, s].reshape(8 * N, 2 * N) for s in range(4)], axis=1)
    weighted = []
    for n in range(G_BLK // step):
        cols = pl.ds(n * step, step)
        picked = jnp.dot(left, column_pick[:, cols], preferred_element_type=F32)
        picked = picked.reshape(8, 4, 16, step)
        halves = []
        for h in range(2):
            factor = twiddle[pl.ds(h * 2 * N, 2 * N), cols].reshape(8, 1, 16, step)
            halves.append(jnp.sum(jnp.sum(picked * factor, axis=0), axis=1))
        values = (jnp.concatenate(halves, axis=0) * (1.0 / (N * 8))).astype(BF16)
        for j in range(32):
            columns[j, :, cols] = values
        weighted.append(weight[...] * values.astype(F32))
    weighted = jnp.concatenate(weighted, axis=1)
    swapped = lax.axis_index("core") == 1
    index = lax.axis_index("y") & 3
    pad = jnp.zeros((8, TAIL - 2 * ROWS), F32)
    tails = []
    for j in range(4):
        rows = weighted[:, j * 2 * ROWS : (j + 1) * 2 * ROWS]
        first, second = rows[:, :ROWS], rows[:, ROWS:]
        mine = jnp.where(swapped, second, first)
        other = jnp.where(swapped, first, second)
        tails.append(jnp.concatenate([mine, pad, other], axis=1))
    for s in range(4):
        part = tails[s]
        for i in range(1, 4):
            part = jnp.where(index == i, tails[(i + s) % 4], part)
        row_parts[s][...] = part.astype(BF16)


def make_elements(slabs, column_pick, twiddle, weight):
    return pl.pallas_call(
        elements_kernel,
        in_specs=[VMEM] * 4,
        out_specs=(VMEM,) * 5,
        out_shape=(jax.ShapeDtypeStruct((32, 8, G_BLK), BF16),) + (pltpu.VMEM((8, TAIL), BF16),) * 4,
        compiler_params=limit(12),
        name="elements",
    )(*in_vmem(slabs, column_pick, twiddle, weight))


def pack_kernel(*refs):
    parts, out = [r[...].astype(F32) for r in refs[:4]], refs[4]
    index = lax.axis_index("y") & 3
    for i in range(4):
        part = parts[(0 - i) % 4]
        for j in range(1, 4):
            part = jnp.where(index == j, parts[(j - i) % 4], part)
        out[i] = part.astype(BF16)


def pack(parts):
    return pl.pallas_call(
        pack_kernel,
        in_specs=[VMEM] * 4,
        out_specs=VMEM,
        out_shape=pltpu.VMEM((4, 8, TAIL), BF16),
        compiler_params=limit(2),
        name="pack",
    )(*in_vmem(*parts))


def spread_kernel(both, out):
    swapped = lax.axis_index("core") == 1
    near = lax.broadcasted_iota(jnp.int32, (8, TAIL), 1) < TAIL // 2
    for i in range(4):
        first, second = both[0, i].astype(F32), both[1, i].astype(F32)
        mine = jnp.where(swapped, second, first)
        other = jnp.where(swapped, first, second)
        rows = jnp.where(near, mine, other).astype(BF16)
        for f in range(8):
            out[f, i] = rows


def spread(both):
    return pl.pallas_call(
        spread_kernel,
        in_specs=[VMEM],
        out_specs=VMEM,
        out_shape=pltpu.VMEM((8, 4, 8, TAIL), BF16),
        compiler_params=limit(2),
        name="spread",
    )(*in_vmem(both))


def left_side(tail, skip):
    rows = tail.astype(F32)
    turned = pltpu.roll(rows.reshape(32, 8, 256), 4, 1)
    sign = jnp.where(lax.broadcasted_iota(jnp.int32, (32, 8, 256), 1) < 4, -1.0, 1.0)
    turned = (turned * sign).reshape(256, 256)
    keep = slice(skip, skip + ROWS)
    return jnp.concatenate([rows.T[keep].astype(BF16), turned.T[keep].astype(BF16)], axis=0)


def product_kernel(rows, mine, other, out, stage, sems):
    left_mine = left_side(rows[:, pl.ds(0, 256)], 0)
    left_other = left_side(rows[:, pl.ds(128, 256)], 96)
    copies = []
    for n in range(5):
        cols = pl.ds(n * 256, 256)
        total = jnp.dot(left_mine, mine[:, cols], preferred_element_type=F32)
        total += jnp.dot(left_other, other[:, cols], preferred_element_type=F32)
        total = total * (1.0 / PAIRS)
        stage[0, :, cols] = total[:ROWS]
        stage[1, :, cols] = total[ROWS:]
        copy = pltpu.make_async_copy(stage.at[:, :, cols], out.at[:, :, cols], sems.at[n])
        copy.start()
        copies.append(copy)
    for copy in copies:
        copy.wait()


def product(rows, mine, other):
    return pl.pallas_call(
        product_kernel,
        in_specs=[VMEM] * 3,
        out_specs=ANY,
        out_shape=jax.ShapeDtypeStruct((2, ROWS, G_BLK), F32),
        scratch_shapes=[pltpu.VMEM((2, ROWS, G_BLK), F32), pltpu.SemaphoreType.DMA((5,))],
        compiler_params=limit(8),
        name="product",
    )(*in_vmem(rows.reshape(256, TAIL), mine.reshape(256, G_BLK), other.reshape(256, G_BLK)))


AXES = ("zh", "y", "core", "x", "zl")


def to_row_owner(part, shift):
    sizes = (4, 8, 2, 4, 2)
    pairs = []
    for source, (zh, y, core, x, zl) in enumerate(np.ndindex(*sizes)):
        target = (x, 4 * zl + (y + shift) % 4, core, zh, y // 4)
        pairs.append((source, int(np.ravel_multi_index(target, sizes))))
    return lax.ppermute(part, AXES, pairs)


def on_device(psi_val, psi_cond, pair_bands, eps_val, eps_cond, g_map):
    z_table, y_table, x_table = host_tables()
    z_tab = jnp.asarray(z_table.astype(np.dtype(BF16)))
    y_tab = jnp.asarray(y_table.astype(np.dtype(BF16)))
    x_tab = jnp.asarray(two_parts(x_table, 1))
    bands = pair_bands.T
    slabs = local_dft(bands, psi_val, psi_cond, z_tab, y_tab)
    slabs = lax.all_to_all(slabs, ("x", "zl"), 0, 0, tiled=True)
    picked = picks(bands, eps_val, eps_cond, g_map.reshape(1, G_BLK), x_tab)
    columns, *row_parts = make_elements(slabs, *picked)
    mine = lax.all_to_all(columns, ("zh", "y"), 0, 0, tiled=True)
    parts = [to_row_owner(part, s) for s, part in enumerate(row_parts)]
    packed = pack(parts)
    both = lax.all_gather(packed[None], "core", axis=0, tiled=True)
    rows = spread(both)
    rows = lax.all_to_all(rows, ("x", "zl"), 0, 0, tiled=True)
    other = lax.ppermute(mine, "core", [(0, 1), (1, 0)])
    return product(rows, mine, other)


def solution(mesh):
    fine = Mesh(mesh.devices.reshape(4, 8, 2, 4, 2), AXES)
    pair, fft = ("zh", "y", "core"), ("x", "zl")
    in_specs = (
        P(pair, fft, None, None),
        P(pair, fft, None, None),
        P(pair, None),
        P(pair),
        P(pair),
        P(fft),
    )
    return jax.shard_map(
        on_device, mesh=fine, in_specs=in_specs, out_specs=P(None, pair, fft), check_vma=False
    )
```

```python
import math

import jax
import jax.numpy as jnp
import numpy as np
from jax import lax
from jax.experimental import pallas as pl
from jax.experimental.pallas import tpu as pltpu
from jax.sharding import Mesh
from jax.sharding import PartitionSpec as P


N = 64
G_BLK = 1280
PAIRS = 256
ROWS = 160
TAIL = 384
F32 = jnp.float32
BF16 = jnp.bfloat16


def host_tables():
    k = np.arange(N)
    angle = 2.0 * math.pi * ((k[:, None] * k[None, :]) % N) / N
    c, s = np.cos(angle), np.sin(angle)
    top = np.concatenate([c, -s, -s, -c], axis=1)
    low = np.concatenate([s, c, c, -s], axis=1)
    z_table = np.concatenate([top, top, low, -low], axis=0)
    order = np.concatenate([k[0::2], k[1::2]])
    y_table = np.concatenate([c, s], axis=1)[order]
    to_re = np.stack([c, s], axis=1).reshape(2 * N, N)
    to_im = np.stack([-s, c], axis=1).reshape(2 * N, N)
    x_table = np.concatenate([to_re, to_im], axis=0)
    return z_table, y_table, x_table


def two_parts(table, axis):
    kind = np.dtype(BF16)
    high = table.astype(kind)
    return np.concatenate([high, (table - high.astype(np.float64)).astype(kind)], axis=axis)


def in_vmem(*arrays):
    return [pltpu.with_memory_space_constraint(a, pltpu.VMEM) for a in arrays]


def limit(mib):
    return pltpu.CompilerParams(vmem_limit_bytes=mib << 20)


SMEM = pl.BlockSpec(memory_space=pltpu.SMEM)
VMEM = pl.BlockSpec(memory_space=pltpu.VMEM)
ANY = pl.BlockSpec(memory_space=pl.ANY)


def local_dft_kernel(bands, val, cond, z_tab, y_tab, out, scratch):
    first = lax.broadcasted_iota(jnp.int32, (N // 2, 2 * N), 1) < N

    def along_z(i):
        v = val[bands[0, i]].reshape(8 * N, 2 * N)
        c = cond[bands[1, i]].reshape(8 * N, 2 * N)
        crossed = jnp.concatenate([c[:, N:], c[:, :N]], axis=1)
        products = jnp.concatenate([v * c, v * crossed], axis=1)
        both = jnp.dot(products, z_tab[...], preferred_element_type=F32)
        return both.astype(BF16)

    def along_y(i, mid):
        parts = []
        for x in range(8):
            rows = mid[x * N : (x + 1) * N]
            parts.append(jnp.concatenate([rows[:, : 2 * N], rows[:, 2 * N :]], axis=0))
        res = jnp.dot(y_tab[...], jnp.concatenate(parts, axis=1), preferred_element_type=F32)
        base = i * 8 * N
        for x in range(8):
            tile = res[:, x * 2 * N : (x + 1) * 2 * N]
            even, odd = tile[: N // 2], tile[N // 2 :]
            scratch[pl.ds(base + x * N, N // 2), :] = jnp.where(first, even, pltpu.roll(odd, N, 1))
            scratch[pl.ds(base + x * N + N // 2, N // 2), :] = jnp.where(first, pltpu.roll(even, N, 1), odd)

    def store(i):
        base = i * 8 * N
        for k in range(N // 2):
            rows = scratch[pl.ds(base + k, 16, stride=N // 2), :]
            out[k // 4, k % 4, pl.ds(16 * i, 16), :] = rows.astype(BF16)

    mids = [along_z(0)]
    for i in range(4):
        if i < 3:
            mids.append(along_z(i + 1))
        along_y(i, mids[i])
        store(i)


def local_dft(bands, psi_val, psi_cond, z_tab, y_tab):
    return pl.pallas_call(
        local_dft_kernel,
        in_specs=[SMEM, VMEM, VMEM, VMEM, VMEM],
        out_specs=VMEM,
        out_shape=pltpu.VMEM((8, 4, N, 2 * N), BF16),
        scratch_shapes=[pltpu.VMEM((4 * 8 * N, 2 * N), F32)],
        name="local_dft",
    )(bands, psi_val, psi_cond, z_tab, y_tab)


def picks_kernel(bands, e_val, e_cond, g_map, x_tab, column_pick, twiddle, weight):
    row = lax.broadcasted_iota(jnp.int32, (8, 256), 0) % 4
    gap = jnp.zeros((8, 256), F32)
    for i in range(4):
        gap = jnp.where(row == i, e_val[bands[0, i]] - e_cond[bands[1, i]], gap)
    weight[...] = 2.0 / gap
    g = g_map[...]
    row = lax.broadcasted_iota(jnp.int32, (8 * N, G_BLK), 0)
    column_pick[...] = jnp.where(row == (g & (8 * N - 1)), 1.0, 0.0).astype(BF16)
    row = lax.broadcasted_iota(jnp.int32, (2 * N, G_BLK), 0)
    x_pick = jnp.where((row & (N - 1)) == (g >> 12), 1.0, 0.0).astype(BF16)
    twiddle[...] = jnp.dot(x_tab[...], x_pick, preferred_element_type=F32)


def picks(bands, eps_val, eps_cond, g_map, x_tab):
    return pl.pallas_call(
        picks_kernel,
        in_specs=[SMEM] * 3 + [VMEM] * 2,
        out_specs=(VMEM,) * 3,
        out_shape=(
            pltpu.VMEM((8 * N, G_BLK), BF16),
            pltpu.VMEM((4 * N, G_BLK), F32),
            pltpu.VMEM((8, 256), F32),
        ),
        compiler_params=limit(8),
        name="picks",
    )(bands, eps_val, eps_cond, g_map, x_tab)


def elements_kernel(slabs, column_pick, twiddle, weight, columns, row_parts):
    step = 256
    left = jnp.concatenate([slabs[:, s].reshape(8 * N, 2 * N) for s in range(4)], axis=1)
    weighted = []
    for n in range(G_BLK // step):
        cols = pl.ds(n * step, step)
        picked = jnp.dot(left, column_pick[:, cols], preferred_element_type=F32)
        picked = picked.reshape(8, 4, 16, step)
        halves = []
        for h in range(2):
            factor = twiddle[pl.ds(h * 2 * N, 2 * N), cols].reshape(8, 1, 16, step)
            halves.append(jnp.sum(jnp.sum(picked * factor, axis=0), axis=1))
        values = (jnp.concatenate(halves, axis=0) * (1.0 / (N * 8))).astype(BF16)
        for j in range(32):
            columns[j, :, cols] = values
        weighted.append(weight[...] * values.astype(F32))
    weighted = jnp.concatenate(weighted, axis=1)
    swapped = lax.axis_index("core") == 1
    pad = jnp.zeros((8, TAIL - 2 * ROWS), F32)
    for j in range(4):
        rows = weighted[:, j * 2 * ROWS : (j + 1) * 2 * ROWS]
        first, second = rows[:, :ROWS], rows[:, ROWS:]
        mine = jnp.where(swapped, second, first)
        other = jnp.where(swapped, first, second)
        row_parts[j] = jnp.concatenate([mine, pad, other], axis=1).astype(BF16)


def make_elements(slabs, column_pick, twiddle, weight):
    return pl.pallas_call(
        elements_kernel,
        in_specs=[VMEM] * 4,
        out_specs=(VMEM, VMEM),
        out_shape=(pltpu.VMEM((32, 8, G_BLK), BF16), pltpu.VMEM((4, 8, TAIL), BF16)),
        compiler_params=limit(12),
        name="elements",
    )(*in_vmem(slabs, column_pick, twiddle, weight))


def spread_kernel(both, out):
    swapped = lax.axis_index("core") == 1
    near = lax.broadcasted_iota(jnp.int32, (8, TAIL), 1) < TAIL // 2
    for i in range(4):
        first, second = both[0, i].astype(F32), both[1, i].astype(F32)
        mine = jnp.where(swapped, second, first)
        other = jnp.where(swapped, first, second)
        rows = jnp.where(near, mine, other).astype(BF16)
        for f in range(8):
            out[f, i] = rows


def spread(both):
    return pl.pallas_call(
        spread_kernel,
        in_specs=[VMEM],
        out_specs=VMEM,
        out_shape=pltpu.VMEM((8, 4, 8, TAIL), BF16),
        compiler_params=limit(2),
        name="spread",
    )(*in_vmem(both))


def left_side(tail, skip):
    rows = tail.astype(F32)
    turned = pltpu.roll(rows.reshape(32, 8, 256), 4, 1)
    sign = jnp.where(lax.broadcasted_iota(jnp.int32, (32, 8, 256), 1) < 4, -1.0, 1.0)
    turned = (turned * sign).reshape(256, 256)
    keep = slice(skip, skip + ROWS)
    return jnp.concatenate([rows.T[keep].astype(BF16), turned.T[keep].astype(BF16)], axis=0)


def product_kernel(rows, mine, other, out, stage, sems):
    order = [(zh ^ 2) * 2 + 1 - half for zh in range(4) for half in range(2)]
    panel = jnp.concatenate([rows[pl.ds(32 * k, 32), :] for k in order], axis=0)
    left_mine = left_side(panel[:, :256], 0)
    left_other = left_side(panel[:, 128:], 96)
    copies = []
    for n in range(5):
        cols = pl.ds(n * 256, 256)
        total = jnp.dot(left_mine, mine[:, cols], preferred_element_type=F32)
        total += jnp.dot(left_other, other[:, cols], preferred_element_type=F32)
        total = total * (1.0 / PAIRS)
        stage[0, :, cols] = total[:ROWS]
        stage[1, :, cols] = total[ROWS:]
        copy = pltpu.make_async_copy(stage.at[:, :, cols], out.at[:, :, cols], sems.at[n])
        copy.start()
        copies.append(copy)
    for copy in copies:
        copy.wait()


def product(rows, mine, other):
    return pl.pallas_call(
        product_kernel,
        in_specs=[VMEM] * 3,
        out_specs=ANY,
        out_shape=jax.ShapeDtypeStruct((2, ROWS, G_BLK), F32),
        scratch_shapes=[pltpu.VMEM((2, ROWS, G_BLK), F32), pltpu.SemaphoreType.DMA((5,))],
        compiler_params=limit(8),
        name="product",
    )(*in_vmem(rows.reshape(256, TAIL), mine.reshape(256, G_BLK), other.reshape(256, G_BLK)))


AXES = ("zh", "yh", "yl", "core", "x", "zl")


def to_row_owner(parts):
    sizes = (4, 2, 4, 2, 4, 2)
    pairs = []
    for source, (zh, yh, yl, core, x, zl) in enumerate(np.ndindex(*sizes)):
        target = (x, zl, yl, core, zh ^ 2, 1 - yh)
        pairs.append((source, int(np.ravel_multi_index(target, sizes))))
    return lax.ppermute(parts, AXES, pairs)


def on_device(psi_val, psi_cond, pair_bands, eps_val, eps_cond, g_map):
    z_table, y_table, x_table = host_tables()
    z_tab = jnp.asarray(z_table.astype(np.dtype(BF16)))
    y_tab = jnp.asarray(y_table.astype(np.dtype(BF16)))
    x_tab = jnp.asarray(two_parts(x_table, 1))
    bands = pair_bands.T
    slabs = local_dft(bands, psi_val, psi_cond, z_tab, y_tab)
    slabs = lax.all_to_all(slabs, ("x", "zl"), 0, 0, tiled=True)
    picked = picks(bands, eps_val, eps_cond, g_map.reshape(1, G_BLK), x_tab)
    columns, row_parts = make_elements(slabs, *picked)
    mine = lax.all_to_all(columns, ("zh", "yh", "yl"), 0, 0, tiled=True)
    parts = to_row_owner(row_parts)
    both = lax.all_gather(parts[None], "core", axis=0, tiled=True)
    rows = spread(both).reshape(32, 8, TAIL)
    rows = lax.all_to_all(rows, ("x", "zl", "yl"), 0, 0, tiled=True)
    other = lax.ppermute(mine, "core", [(0, 1), (1, 0)])
    return product(rows, mine, other)


def solution(mesh):
    fine = Mesh(mesh.devices.reshape(4, 2, 4, 2, 4, 2), AXES)
    pair, fft = ("zh", "yh", "yl", "core"), ("x", "zl")
    in_specs = (
        P(pair, fft, None, None),
        P(pair, fft, None, None),
        P(pair, None),
        P(pair),
        P(pair),
        P(fft),
    )
    return jax.shard_map(
        on_device, mesh=fine, in_specs=in_specs, out_specs=P(None, pair, fft), check_vma=False
    )
```

```python
import math

import jax
import jax.numpy as jnp
import numpy as np
from jax import lax
from jax.experimental import pallas as pl
from jax.experimental.pallas import tpu as pltpu
from jax.sharding import Mesh
from jax.sharding import PartitionSpec as P

N = 64
G_BLK = 1280
PITCH = 33
PAIRS = 256
ROWS = 160
MSG = 1664
F32 = jnp.float32
BF16 = jnp.bfloat16


def host_tables():
    k = np.arange(N)
    angle = 2.0 * math.pi * ((k[:, None] * k[None, :]) % N) / N
    c, s = np.cos(angle), np.sin(angle)
    top = np.concatenate([c, -s, -s, -c], axis=1)
    low = np.concatenate([s, c, c, -s], axis=1)
    z_table = np.concatenate([top, top, low, -low], axis=0)
    order = np.concatenate([k[0::2], k[1::2]])
    y_table = np.concatenate([c, s], axis=1)[order]
    to_re = np.stack([c, s], axis=1).reshape(2 * N, N)
    to_im = np.stack([-s, c], axis=1).reshape(2 * N, N)
    x_table = np.concatenate([to_re, to_im], axis=0)
    return z_table, y_table, x_table


def two_parts(table, axis):
    kind = np.dtype(BF16)
    high = table.astype(kind)
    return np.concatenate([high, (table - high.astype(np.float64)).astype(kind)], axis=axis)


def in_vmem(*arrays):
    return [pltpu.with_memory_space_constraint(a, pltpu.VMEM) for a in arrays]


def limit(mib):
    return pltpu.CompilerParams(vmem_limit_bytes=mib << 20)


SMEM = pl.BlockSpec(memory_space=pltpu.SMEM)
VMEM = pl.BlockSpec(memory_space=pltpu.VMEM)
ANY = pl.BlockSpec(memory_space=pl.ANY)


def local_dft_kernel(bands, val, cond, z_tab, y_tab, out, scratch):
    first = lax.broadcasted_iota(jnp.int32, (N // 2, 2 * N), 1) < N

    def along_z(i):
        v = val[bands[0, i]].reshape(8 * N, 2 * N)
        c = cond[bands[1, i]].reshape(8 * N, 2 * N)
        crossed = jnp.concatenate([c[:, N:], c[:, :N]], axis=1)
        products = jnp.concatenate([v * c, v * crossed], axis=1)
        both = jnp.dot(products, z_tab[...], preferred_element_type=F32)
        return both.astype(BF16)

    def along_y(i, mid):
        parts = []
        for x in range(8):
            rows = mid[x * N : (x + 1) * N]
            parts.append(jnp.concatenate([rows[:, : 2 * N], rows[:, 2 * N :]], axis=0))
        res = jnp.dot(y_tab[...], jnp.concatenate(parts, axis=1), preferred_element_type=F32)
        base = i * 16 * PITCH
        for x in range(8):
            tile = res[:, x * 2 * N : (x + 1) * 2 * N]
            even, odd = tile[: N // 2], tile[N // 2 :]
            turned = pltpu.roll(jnp.where(first, odd, even), N, 1)
            scratch[pl.ds(base + 2 * x * PITCH, N // 2), :] = jnp.where(first, even, turned)
            scratch[pl.ds(base + (2 * x + 1) * PITCH, N // 2), :] = jnp.where(first, turned, odd)

    def store(i):
        base = i * 16 * PITCH
        for k in range(N // 2):
            rows = scratch[pl.ds(base + k, 16, stride=PITCH), :]
            out[k // 4, k % 4, pl.ds(16 * i, 16), :] = rows.astype(BF16)

    mids = [along_z(0)]
    for i in range(4):
        if i < 3:
            mids.append(along_z(i + 1))
        along_y(i, mids[i])
        store(i)


def local_dft(bands, psi_val, psi_cond, z_tab, y_tab):
    return pl.pallas_call(
        local_dft_kernel,
        in_specs=[SMEM, VMEM, VMEM, VMEM, VMEM],
        out_specs=VMEM,
        out_shape=pltpu.VMEM((8, 4, N, 2 * N), BF16),
        scratch_shapes=[pltpu.VMEM((4 * 16 * PITCH, 2 * N), F32)],
        name="local_dft",
    )(bands, psi_val, psi_cond, z_tab, y_tab)


def picks_kernel(bands, e_val, e_cond, g_map, x_tab, column_pick, twiddle, weight):
    row = lax.broadcasted_iota(jnp.int32, (8, 256), 0) % 4
    gap = jnp.zeros((8, 256), F32)
    for i in range(4):
        gap = jnp.where(row == i, e_val[bands[0, i]] - e_cond[bands[1, i]], gap)
    weight[...] = 2.0 / gap
    g = g_map[...]
    row = lax.broadcasted_iota(jnp.int32, (8 * N, G_BLK), 0)
    column_pick[...] = jnp.where(row == (g & (8 * N - 1)), 1.0, 0.0).astype(BF16)
    row = lax.broadcasted_iota(jnp.int32, (2 * N, G_BLK), 0)
    x_pick = jnp.where((row & (N - 1)) == (g >> 12), 1.0, 0.0).astype(BF16)
    twiddle[...] = jnp.dot(x_tab[...], x_pick, preferred_element_type=F32)


def picks(bands, eps_val, eps_cond, g_map, x_tab):
    return pl.pallas_call(
        picks_kernel,
        in_specs=[SMEM] * 3 + [VMEM] * 2,
        out_specs=(VMEM,) * 3,
        out_shape=(
            pltpu.VMEM((8 * N, G_BLK), BF16),
            pltpu.VMEM((4 * N, G_BLK), F32),
            pltpu.VMEM((8, 256), F32),
        ),
        compiler_params=limit(8),
        name="picks",
    )(bands, eps_val, eps_cond, g_map, x_tab)


def elements_kernel(slabs, column_pick, twiddle, weight, elements, scaled):
    step = 256
    left = jnp.concatenate([slabs[:, s].reshape(8 * N, 2 * N) for s in range(4)], axis=1)
    for n in range(G_BLK // step):
        cols = pl.ds(n * step, step)
        picked = jnp.dot(left, column_pick[:, cols], preferred_element_type=F32)
        picked = picked.reshape(8, 4, 16, step)
        halves = []
        for h in range(2):
            factor = twiddle[pl.ds(h * 2 * N, 2 * N), cols].reshape(8, 1, 16, step)
            halves.append(jnp.sum(jnp.sum(picked * factor, axis=0), axis=1))
        values = (jnp.concatenate(halves, axis=0) * (1.0 / (N * 8))).astype(BF16)
        elements[:, cols] = values
        weighted = (weight[...] * values.astype(F32)).astype(BF16)
        for f in range(8):
            scaled[f, :, cols] = weighted


def make_elements(slabs, column_pick, twiddle, weight):
    return pl.pallas_call(
        elements_kernel,
        in_specs=[VMEM] * 4,
        out_specs=(VMEM, VMEM),
        out_shape=(pltpu.VMEM((8, G_BLK), BF16), pltpu.VMEM((8, 8, G_BLK), BF16)),
        compiler_params=limit(12),
        name="elements",
    )(*in_vmem(slabs, column_pick, twiddle, weight))


def messages_kernel(elements, scaled, out):
    swapped = lax.axis_index("core") == 1
    values = elements[...]
    pad = jnp.zeros((8, MSG - G_BLK - 2 * ROWS), F32)
    for j in range(32):
        out[j, :, pl.ds(0, G_BLK)] = values
        part = (j % 4) * 2 * ROWS
        rows = scaled[j // 4].astype(F32)[:, part : part + 2 * ROWS]
        first, second = rows[:, :ROWS], rows[:, ROWS:]
        mine = jnp.where(swapped, second, first)
        other = jnp.where(swapped, first, second)
        tail = jnp.concatenate([mine, pad, other], axis=1).astype(BF16)
        out[j, :, pl.ds(G_BLK, MSG - G_BLK)] = tail


def make_messages(elements, scaled):
    return pl.pallas_call(
        messages_kernel,
        in_specs=[VMEM, VMEM],
        out_specs=VMEM,
        out_shape=pltpu.VMEM((32, 8, MSG), BF16),
        compiler_params=limit(4),
        name="messages",
    )(*in_vmem(elements, scaled))


def left_side(tail, skip):
    rows = tail.astype(F32)
    turned = pltpu.roll(rows.reshape(32, 8, 256), 4, 1)
    sign = jnp.where(lax.broadcasted_iota(jnp.int32, (32, 8, 256), 1) < 4, -1.0, 1.0)
    turned = (turned * sign).reshape(256, 256)
    keep = slice(skip, skip + ROWS)
    return jnp.concatenate([rows.T[keep].astype(BF16), turned.T[keep].astype(BF16)], axis=0)


def first_half_kernel(data, out):
    left = left_side(data[:, pl.ds(G_BLK, 256)], 0)
    for n in range(5):
        cols = pl.ds(n * 256, 256)
        out[:, cols] = jnp.dot(left, data[:, cols], preferred_element_type=F32)


def first_half(data):
    return pl.pallas_call(
        first_half_kernel,
        in_specs=[VMEM],
        out_specs=VMEM,
        out_shape=pltpu.VMEM((2 * ROWS, G_BLK), F32),
        compiler_params=limit(8),
        name="first_half",
    )(*in_vmem(data.reshape(256, MSG)))


def second_half_kernel(data, start, out, stage, sems):
    left = left_side(data[:, pl.ds(G_BLK + 128, 256)], 96)
    copies = []
    for n in range(5):
        cols = pl.ds(n * 256, 256)
        total = start[:, cols] + jnp.dot(left, data[:, cols], preferred_element_type=F32)
        total = total * (1.0 / PAIRS)
        stage[0, :, cols] = total[:ROWS]
        stage[1, :, cols] = total[ROWS:]
        copy = pltpu.make_async_copy(stage.at[:, :, cols], out.at[:, :, cols], sems.at[n])
        copy.start()
        copies.append(copy)
    for copy in copies:
        copy.wait()


def second_half(data, start):
    return pl.pallas_call(
        second_half_kernel,
        in_specs=[VMEM, VMEM],
        out_specs=ANY,
        out_shape=jax.ShapeDtypeStruct((2, ROWS, G_BLK), F32),
        scratch_shapes=[pltpu.VMEM((2, ROWS, G_BLK), F32), pltpu.SemaphoreType.DMA((5,))],
        compiler_params=limit(8),
        name="second_half",
    )(*in_vmem(data.reshape(256, MSG), start))


def on_device(psi_val, psi_cond, pair_bands, eps_val, eps_cond, g_map):
    z_table, y_table, x_table = host_tables()
    z_tab = jnp.asarray(z_table.astype(np.dtype(BF16)))
    y_tab = jnp.asarray(y_table.astype(np.dtype(BF16)))
    x_tab = jnp.asarray(two_parts(x_table, 1))
    bands = pair_bands.T
    slabs = local_dft(bands, psi_val, psi_cond, z_tab, y_tab)
    slabs = lax.all_to_all(slabs, ("x", "zl"), 0, 0, tiled=True)
    picked = picks(bands, eps_val, eps_cond, g_map.reshape(1, G_BLK), x_tab)
    elements, scaled = make_elements(slabs, *picked)
    scaled = lax.all_to_all(scaled, ("x", "zl"), 0, 0, tiled=True)
    data = make_messages(elements, scaled)
    mine = lax.all_to_all(data, ("zh", "y"), 0, 0, tiled=True)
    other = lax.ppermute(mine, "core", [(0, 1), (1, 0)])
    return second_half(other, first_half(mine))


def solution(mesh):
    fine = Mesh(mesh.devices.reshape(4, 8, 2, 4, 2), ("zh", "y", "core", "x", "zl"))
    pair, fft = ("zh", "y", "core"), ("x", "zl")
    in_specs = (
        P(pair, fft, None, None),
        P(pair, fft, None, None),
        P(pair, None),
        P(pair),
        P(pair),
        P(fft),
    )
    return jax.shard_map(
        on_device, mesh=fine, in_specs=in_specs, out_specs=P(None, pair, fft), check_vma=False
    )
```

```python
import math

import jax
import jax.numpy as jnp
import numpy as np
from jax import lax
from jax.experimental import pallas as pl
from jax.experimental.pallas import tpu as pltpu
from jax.sharding import Mesh
from jax.sharding import PartitionSpec as P

N = 64
G_BLK = 1280
PITCH = 33
PAIRS = 256
ROWS = 160
MSG = 1664
F32 = jnp.float32
BF16 = jnp.bfloat16


def host_tables():
    k = np.arange(N)
    angle = 2.0 * math.pi * ((k[:, None] * k[None, :]) % N) / N
    c, s = np.cos(angle), np.sin(angle)
    top = np.concatenate([c, -s, -s, -c], axis=1)
    low = np.concatenate([s, c, c, -s], axis=1)
    z_table = np.concatenate([top, top, low, -low], axis=0)
    order = np.concatenate([k[0::2], k[1::2]])
    y_table = np.concatenate([c, s], axis=1)[order]
    to_re = np.stack([c, s], axis=1).reshape(2 * N, N)
    to_im = np.stack([-s, c], axis=1).reshape(2 * N, N)
    x_table = np.concatenate([to_re, to_im], axis=0)
    return z_table, y_table, x_table


def two_parts(table, axis):
    kind = np.dtype(BF16)
    high = table.astype(kind)
    return np.concatenate([high, (table - high.astype(np.float64)).astype(kind)], axis=axis)


def in_vmem(*arrays):
    return [pltpu.with_memory_space_constraint(a, pltpu.VMEM) for a in arrays]


def limit(mib):
    return pltpu.CompilerParams(vmem_limit_bytes=mib << 20)


SMEM = pl.BlockSpec(memory_space=pltpu.SMEM)
VMEM = pl.BlockSpec(memory_space=pltpu.VMEM)
ANY = pl.BlockSpec(memory_space=pl.ANY)


def local_dft_kernel(bands, val, cond, z_tab, y_tab, out, scratch, stage, sems):
    first = lax.broadcasted_iota(jnp.int32, (N // 2, 2 * N), 1) < N

    def along_z(i):
        v = val[bands[0, i]].reshape(8 * N, 2 * N)
        c = cond[bands[1, i]].reshape(8 * N, 2 * N)
        crossed = jnp.concatenate([c[:, N:], c[:, :N]], axis=1)
        products = jnp.concatenate([v * c, v * crossed], axis=1)
        both = jnp.dot(products, z_tab[...], preferred_element_type=F32)
        return both.astype(BF16)

    def along_y(i, mid):
        parts = []
        for x in range(8):
            rows = mid[x * N : (x + 1) * N]
            parts.append(jnp.concatenate([rows[:, : 2 * N], rows[:, 2 * N :]], axis=0))
        res = jnp.dot(y_tab[...], jnp.concatenate(parts, axis=1), preferred_element_type=F32)
        base = i * 16 * PITCH
        for x in range(8):
            tile = res[:, x * 2 * N : (x + 1) * 2 * N]
            even, odd = tile[: N // 2], tile[N // 2 :]
            turned = pltpu.roll(jnp.where(first, odd, even), N, 1)
            scratch[pl.ds(base + 2 * x * PITCH, N // 2), :] = jnp.where(first, even, turned)
            scratch[pl.ds(base + (2 * x + 1) * PITCH, N // 2), :] = jnp.where(first, turned, odd)

    def store(i):
        base = i * 16 * PITCH
        for k in range(N // 2):
            rows = scratch[pl.ds(base + k, 16, stride=PITCH), :]
            stage[k // 4, k % 4, pl.ds(16 * i, 16), :] = rows.astype(BF16)
        part = (slice(None), slice(None), pl.ds(16 * i, 16))
        copies.append(pltpu.make_async_copy(stage.at[part], out.at[part], sems.at[i]))
        copies[-1].start()

    copies = []
    mids = [along_z(0)]
    for i in range(4):
        if i < 3:
            mids.append(along_z(i + 1))
        along_y(i, mids[i])
        store(i)
    for copy in copies:
        copy.wait()


def local_dft(bands, psi_val, psi_cond, z_tab, y_tab):
    return pl.pallas_call(
        local_dft_kernel,
        in_specs=[SMEM, VMEM, VMEM, VMEM, VMEM],
        out_specs=ANY,
        out_shape=jax.ShapeDtypeStruct((8, 4, N, 2 * N), BF16),
        scratch_shapes=[
            pltpu.VMEM((4 * 16 * PITCH, 2 * N), F32),
            pltpu.VMEM((8, 4, N, 2 * N), BF16),
            pltpu.SemaphoreType.DMA((4,)),
        ],
        name="local_dft",
    )(bands, psi_val, psi_cond, z_tab, y_tab)


def picks_kernel(bands, e_val, e_cond, g_map, x_tab, column_pick, twiddle, weight):
    row = lax.broadcasted_iota(jnp.int32, (8, 256), 0) % 4
    gap = jnp.zeros((8, 256), F32)
    for i in range(4):
        gap = jnp.where(row == i, e_val[bands[0, i]] - e_cond[bands[1, i]], gap)
    weight[...] = 2.0 / gap
    g = g_map[...]
    row = lax.broadcasted_iota(jnp.int32, (8 * N, G_BLK), 0)
    column_pick[...] = jnp.where(row == (g & (8 * N - 1)), 1.0, 0.0).astype(BF16)
    row = lax.broadcasted_iota(jnp.int32, (2 * N, G_BLK), 0)
    x_pick = jnp.where((row & (N - 1)) == (g >> 12), 1.0, 0.0).astype(BF16)
    twiddle[...] = jnp.dot(x_tab[...], x_pick, preferred_element_type=F32)


def picks(bands, eps_val, eps_cond, g_map, x_tab):
    return pl.pallas_call(
        picks_kernel,
        in_specs=[SMEM] * 3 + [VMEM] * 2,
        out_specs=(VMEM,) * 3,
        out_shape=(
            pltpu.VMEM((8 * N, G_BLK), BF16),
            pltpu.VMEM((4 * N, G_BLK), F32),
            pltpu.VMEM((8, 256), F32),
        ),
        compiler_params=limit(8),
        name="picks",
    )(bands, eps_val, eps_cond, g_map, x_tab)


def elements_kernel(slabs, column_pick, twiddle, weight, elements, scaled):
    step = 256
    left = jnp.concatenate([slabs[:, s].reshape(8 * N, 2 * N) for s in range(4)], axis=1)
    for n in range(G_BLK // step):
        cols = pl.ds(n * step, step)
        picked = jnp.dot(left, column_pick[:, cols], preferred_element_type=F32)
        picked = picked.reshape(8, 4, 16, step)
        halves = []
        for h in range(2):
            factor = twiddle[pl.ds(h * 2 * N, 2 * N), cols].reshape(8, 1, 16, step)
            halves.append(jnp.sum(jnp.sum(picked * factor, axis=0), axis=1))
        values = (jnp.concatenate(halves, axis=0) * (1.0 / (N * 8))).astype(BF16)
        elements[:, cols] = values
        weighted = (weight[...] * values.astype(F32)).astype(BF16)
        for f in range(8):
            scaled[f, :, cols] = weighted


def make_elements(slabs, column_pick, twiddle, weight):
    return pl.pallas_call(
        elements_kernel,
        in_specs=[VMEM] * 4,
        out_specs=(VMEM, VMEM),
        out_shape=(pltpu.VMEM((8, G_BLK), BF16), pltpu.VMEM((8, 8, G_BLK), BF16)),
        compiler_params=limit(12),
        name="elements",
    )(*in_vmem(slabs, column_pick, twiddle, weight))


def messages_kernel(elements, scaled, out):
    swapped = lax.axis_index("core") == 1
    values = elements[...]
    pad = jnp.zeros((8, MSG - G_BLK - 2 * ROWS), F32)
    for j in range(32):
        out[j, :, pl.ds(0, G_BLK)] = values
        part = (j % 4) * 2 * ROWS
        rows = scaled[j // 4].astype(F32)[:, part : part + 2 * ROWS]
        first, second = rows[:, :ROWS], rows[:, ROWS:]
        mine = jnp.where(swapped, second, first)
        other = jnp.where(swapped, first, second)
        tail = jnp.concatenate([mine, pad, other], axis=1).astype(BF16)
        out[j, :, pl.ds(G_BLK, MSG - G_BLK)] = tail


def make_messages(elements, scaled):
    return pl.pallas_call(
        messages_kernel,
        in_specs=[VMEM, VMEM],
        out_specs=VMEM,
        out_shape=pltpu.VMEM((32, 8, MSG), BF16),
        compiler_params=limit(4),
        name="messages",
    )(*in_vmem(elements, scaled))


def left_side(tail, skip):
    rows = tail.astype(F32)
    turned = pltpu.roll(rows.reshape(32, 8, 256), 4, 1)
    sign = jnp.where(lax.broadcasted_iota(jnp.int32, (32, 8, 256), 1) < 4, -1.0, 1.0)
    turned = (turned * sign).reshape(256, 256)
    keep = slice(skip, skip + ROWS)
    return jnp.concatenate([rows.T[keep].astype(BF16), turned.T[keep].astype(BF16)], axis=0)


def first_half_kernel(data, out):
    left = left_side(data[:, pl.ds(G_BLK, 256)], 0)
    for n in range(5):
        cols = pl.ds(n * 256, 256)
        out[:, cols] = jnp.dot(left, data[:, cols], preferred_element_type=F32)


def first_half(data):
    return pl.pallas_call(
        first_half_kernel,
        in_specs=[VMEM],
        out_specs=VMEM,
        out_shape=pltpu.VMEM((2 * ROWS, G_BLK), F32),
        compiler_params=limit(8),
        name="first_half",
    )(*in_vmem(data.reshape(256, MSG)))


def second_half_kernel(data, start, out, stage, sems):
    left = left_side(data[:, pl.ds(G_BLK + 128, 256)], 96)
    copies = []
    for n in range(5):
        cols = pl.ds(n * 256, 256)
        total = start[:, cols] + jnp.dot(left, data[:, cols], preferred_element_type=F32)
        total = total * (1.0 / PAIRS)
        stage[0, :, cols] = total[:ROWS]
        stage[1, :, cols] = total[ROWS:]
        copy = pltpu.make_async_copy(stage.at[:, :, cols], out.at[:, :, cols], sems.at[n])
        copy.start()
        copies.append(copy)
    for copy in copies:
        copy.wait()


def second_half(data, start):
    return pl.pallas_call(
        second_half_kernel,
        in_specs=[VMEM, VMEM],
        out_specs=ANY,
        out_shape=jax.ShapeDtypeStruct((2, ROWS, G_BLK), F32),
        scratch_shapes=[pltpu.VMEM((2, ROWS, G_BLK), F32), pltpu.SemaphoreType.DMA((5,))],
        compiler_params=limit(8),
        name="second_half",
    )(*in_vmem(data.reshape(256, MSG), start))


def on_device(psi_val, psi_cond, pair_bands, eps_val, eps_cond, g_map):
    z_table, y_table, x_table = host_tables()
    z_tab = jnp.asarray(z_table.astype(np.dtype(BF16)))
    y_tab = jnp.asarray(y_table.astype(np.dtype(BF16)))
    x_tab = jnp.asarray(two_parts(x_table, 1))
    bands = pair_bands.T
    slabs = local_dft(bands, psi_val, psi_cond, z_tab, y_tab)
    slabs = lax.all_to_all(slabs, ("x", "zl"), 0, 0, tiled=True)
    picked = picks(bands, eps_val, eps_cond, g_map.reshape(1, G_BLK), x_tab)
    elements, scaled = make_elements(slabs, *picked)
    scaled = lax.all_to_all(scaled, ("x", "zl"), 0, 0, tiled=True)
    data = make_messages(elements, scaled)
    mine = lax.all_to_all(data, ("zh", "y"), 0, 0, tiled=True)
    other = lax.ppermute(mine, "core", [(0, 1), (1, 0)])
    return second_half(other, first_half(mine))


def solution(mesh):
    fine = Mesh(mesh.devices.reshape(4, 8, 2, 4, 2), ("zh", "y", "core", "x", "zl"))
    pair, fft = ("zh", "y", "core"), ("x", "zl")
    in_specs = (
        P(pair, fft, None, None),
        P(pair, fft, None, None),
        P(pair, None),
        P(pair),
        P(pair),
        P(fft),
    )
    return jax.shard_map(
        on_device, mesh=fine, in_specs=in_specs, out_specs=P(None, pair, fft), check_vma=False
    )
```
